512 devices in a mesh: gz: 32 (over x_hi, z, core), gy: 16 (over x_lo, y).
Axes of the slice: x: 4 (x_hi: 2, x_lo: 2; x = x_hi * 2 + x_lo), y: 8, z: 8, core: 2. Of those that a mesh axis runs over, the one named last changes fastest.
Arguments:
- tokens: bfloat16 [1, 64, 32, 64, 512], P(None, 'gz', 'gy'), may hold values from -75 to 75
- w_qkv: bfloat16 [512, 1536], replicated, may hold values from -0.25 to 0.25
- w_out: bfloat16 [512, 512], replicated, may hold values from -0.25 to 0.25
- rel_bias: float32 [16, 5, 5, 5], replicated, may hold values from -4 to 4
- gain: float32 [512], replicated, may hold values from 0.5 to 1.5
Outputs:
- update: bfloat16 [1, 64, 32, 64, 512], P(None, 'gz', 'gy')
The draws below stay inside these ranges and needn't reach their ends.
All inputs are finite; a program needn't handle non-finite values.
Results may differ from the reference program's by a relative error of at most 0.0079.
Values may be sent and summed in bfloat16 or wider, within the bound.
No kernel may reach another device: no remote copies, remote signals or barrier semaphores. Data moves between devices by JAX's collectives and lax.ppermute only.
A program may use at most 128 MiB of HBM per device.

```python
import jax
import jax.numpy as jnp
from jax import lax

D = 512
H = 16
HD = 32
KERNEL = 5
DILATION_DEPTH = 8
XLEN = 64
BOX = 1
DEPTH_TOKENS = 64
YLEN = 32


def draw_tokens(key, part):
    full_shape = (BOX, DEPTH_TOKENS, YLEN, XLEN, D)
    key_base = jax.random.fold_in(key, 0)
    result = jnp.clip(jax.random.normal(key_base, full_shape, jnp.float32), -6.0, 6.0)
    return result.astype(jnp.bfloat16)


def bell_draw(stream_key, dims, scale, limit, held_as=jnp.bfloat16):
    return jnp.clip(scale * jax.random.normal(stream_key, dims, jnp.float32), -limit, limit).astype(held_as)


def setup_inputs(seed: int = 0) -> dict:
    streams_of = jax.random.split(jax.random.key(seed), 6)
    return {
        "tokens": draw_tokens(jax.random.fold_in(streams_of[5], 71), 0),
        "w_qkv": bell_draw(streams_of[1], (D, 3 * D), D ** -0.5, 0.25),
        "w_out": bell_draw(streams_of[2], (D, D), D ** -0.5, 0.25),
        "rel_bias": bell_draw(streams_of[3], (H, KERNEL, KERNEL, KERNEL), 1.0, 4.0, jnp.float32),
        "gain": jnp.clip(1.0 + 0.1 * jax.random.normal(streams_of[4], (D,), jnp.float32), 0.5, 1.5),
    }


def reference(tokens, w_qkv, w_out, rel_bias, gain):
    kernel_radius = KERNEL // 2
    flat_tokens = tokens.reshape(-1, D)
    projected = jnp.dot(flat_tokens, w_qkv, preferred_element_type=jnp.float32).astype(jnp.bfloat16)
    projected = projected.reshape(BOX, DEPTH_TOKENS, YLEN, XLEN, H, 3, HD)
    score_scale = float(HD) ** (-0.5)

    def one_plane(depth_plane_index):
        own_plane = lax.dynamic_index_in_dim(projected, depth_plane_index, 1, keepdims=False)
        queries = own_plane[..., 0, :].astype(jnp.float32)
        scores = []
        for depth_tap in range(KERNEL):
            source_plane = (depth_plane_index + DILATION_DEPTH * (depth_tap - kernel_radius)) % DEPTH_TOKENS
            key_plane = lax.dynamic_index_in_dim(projected, source_plane, 1, keepdims=False)
            for tap_y in range(KERNEL):
                for tap_x in range(KERNEL):
                    shifted = jnp.roll(key_plane, (kernel_radius - tap_y, kernel_radius - tap_x), axis=(1, 2))
                    dotted = lax.optimization_barrier(jnp.sum(queries * shifted[..., 1, :].astype(jnp.float32), axis=-1))
                    scores.append(dotted * score_scale + rel_bias[:, depth_tap, tap_y, tap_x])
        stacked = jnp.stack(scores, -1)
        row_max = lax.optimization_barrier(jnp.max(stacked, axis=-1, keepdims=True))
        exponent = jnp.exp(stacked - row_max)
        weights = (exponent / lax.optimization_barrier(jnp.sum(exponent, axis=-1, keepdims=True))).astype(jnp.bfloat16)
        summed = jnp.zeros(queries.shape, jnp.float32)
        position = 0
        for depth_tap in range(KERNEL):
            source_plane = (depth_plane_index + DILATION_DEPTH * (depth_tap - kernel_radius)) % DEPTH_TOKENS
            key_plane = lax.dynamic_index_in_dim(projected, source_plane, 1, keepdims=False)
            for tap_y in range(KERNEL):
                for tap_x in range(KERNEL):
                    shifted = jnp.roll(key_plane, (kernel_radius - tap_y, kernel_radius - tap_x), axis=(1, 2))
                    summed = summed + weights[..., position, None].astype(jnp.float32) * shifted[..., 2, :].astype(jnp.float32)
                    position = position + 1
        return summed.astype(jnp.bfloat16).reshape(BOX, YLEN, XLEN, D)
    per_plane = lax.map(one_plane, jnp.arange(DEPTH_TOKENS, dtype=jnp.int32))
    attended = jnp.moveaxis(per_plane, 0, 1)
    projection = jnp.dot(attended.reshape(-1, D), w_out, preferred_element_type=jnp.float32)
    mean_sq = lax.optimization_barrier(jnp.mean(projection * projection, axis=-1, keepdims=True))
    update = projection * lax.rsqrt(mean_sq + 1e-06) * gain
    return update.astype(jnp.bfloat16).reshape(BOX, DEPTH_TOKENS, YLEN, XLEN, D)
```

```python
import functools
import math

import jax
import jax.numpy as jnp
import numpy as np
from jax import lax
from jax.experimental import pallas as pl
from jax.experimental.pallas import tpu as pltpu
from jax.sharding import PartitionSpec as P


DILATION_DEPTH = 8
LOG2E = math.log2(math.e)
MASKED = -1e30
GROUP = 4
CHAINS = 64


def product_nt(a, b):
    return lax.dot_general(a, b, (((1,), (1,)), ((), ())), preferred_element_type=jnp.float32)


def shifted(block, axis, distance):
    count = lax.axis_size(axis)
    return lax.ppermute(block, axis, [((i - distance) % count, i) for i in range(count)])


def weight_kernel(head_dim, w_ref, query_ref, key_ref, value_ref):
    wide = GROUP * head_dim
    rows = lax.broadcasted_iota(jnp.int32, (wide, 3 * wide), 0)
    columns = lax.broadcasted_iota(jnp.int32, (wide, 3 * wide), 1)
    for group in range(key_ref.shape[0] // wide):
        block = w_ref[:, group * 3 * wide : (group + 1) * 3 * wide]
        for kind, ref in enumerate((query_ref, key_ref, value_ref)):
            source = (rows // head_dim) * 3 * head_dim + kind * head_dim + rows % head_dim
            pick = jnp.where(columns == source, 1.0, 0.0).astype(jnp.bfloat16)
            where = slice(group * wide, (group + 1) * wide)
            if kind == 1:
                ref[:, where] = product_nt(block, pick).astype(jnp.bfloat16)
            else:
                ref[where, :] = product_nt(pick, block).astype(jnp.bfloat16)


def split_weights(w_qkv, head_dim):
    width = w_qkv.shape[0]
    one = pltpu.VMEM((width, width), jnp.bfloat16)
    return pl.pallas_call(
        functools.partial(weight_kernel, head_dim),
        out_shape=[one] * 3,
        cost_estimate=pl.CostEstimate(
            flops=3_000_000_000, transcendentals=0, bytes_accessed=3_000_000
        ),
        name="split_weights",
    )(w_qkv)


def bias_rows(rel_bias, y_rows, cells):
    heads, taps, kernel, _ = rel_bias.shape
    radius = kernel // 2
    key_rows = y_rows + kernel - 1
    lanes = y_rows * cells
    place = np.zeros((kernel, kernel, key_rows, cells, y_rows), np.float32)
    for key_row in range(key_rows):
        for q in range(y_rows):
            if 0 <= key_row - q < kernel:
                for k in range(kernel):
                    place[key_row - q, k, key_row, (radius - k) % cells, q] = 1.0
    place = place.reshape(kernel * kernel, key_rows * lanes)
    outside = np.where(place.sum(0) > 0, 0.0, MASKED).astype(np.float32)
    rows = jnp.dot(
        rel_bias.reshape(heads * taps, kernel * kernel),
        jnp.asarray(place),
        precision=lax.Precision.HIGHEST,
    )
    return rows * LOG2E + jnp.asarray(outside)


def stage_kernel(which, kernel, cells, first, last, scale, *refs):
    refs = list(refs)
    own_ref, low_ref, high_ref, wk_ref, wv_ref, bias_ref = refs[:6]
    refs = refs[6:]
    if first:
        wq_ref = refs.pop(0)
    else:
        query_in, acc_in, max_in, sum_in = refs[:4]
        refs = refs[4:]
    if last:
        wo_ref, gain_ref, out_ref = refs[:3]
        refs = refs[3:]
    else:
        if first:
            query_out = refs.pop(0)
        acc_out, max_out, sum_out = refs[:3]
        refs = refs[3:]
    keys_ref, values_ref, score_ref, spread_ref = refs[:4]
    refs = refs[4:]
    if last:
        attended_ref = refs[0]
    query_ref = query_out if first else query_in
    taps = len(which)
    planes = own_ref.shape[0] // taps
    tokens = own_ref.shape[1]
    y_rows = tokens // cells
    head_dim = 32
    group = pl.program_id(0)

    def reorder(a, side):
        order = jnp.where(interleave, 1.0, 0.0).astype(jnp.bfloat16)
        moved = lax.dot_general(
            a, order, (((1,), (side,)), ((), ())), preferred_element_type=jnp.float32
        )
        return moved.astype(jnp.bfloat16)

    from_lane = lax.broadcasted_iota(jnp.int32, (tokens, tokens), 0)
    to_lane = lax.broadcasted_iota(jnp.int32, (tokens, tokens), 1)
    interleave = from_lane == (to_lane % y_rows) * cells + to_lane // y_rows

    @pl.when(group == 0)
    def _():
        for part, ref in enumerate((low_ref, own_ref, high_ref)):
            block = ref[...].reshape(taps * planes * tokens, ref.shape[2])
            keys = jnp.dot(block, wk_ref[...], preferred_element_type=jnp.float32)
            values = product_nt(wv_ref[...], block)
            for tap in range(taps):
                for plane in range(planes):
                    start = (tap * 3 + part) * tokens
                    at = (tap * planes + plane) * tokens
                    keys_ref[plane, start : start + tokens, :] = keys[
                        at : at + tokens
                    ].astype(jnp.bfloat16)
                    values_ref[plane, :, start : start + tokens] = values[
                        :, at : at + tokens
                    ].astype(jnp.bfloat16)
        if first:
            queries = product_nt(wq_ref[...], own_ref[...].reshape(planes * tokens, own_ref.shape[2]))
            for plane in range(planes):
                query_out[plane] = reorder(
                    queries[:, plane * tokens : (plane + 1) * tokens].astype(jnp.bfloat16), 0
                )

    wide = GROUP * head_dim
    base = pl.multiple_of(group * wide, wide)
    count = keys_ref.shape[1]
    head_of_row = lax.broadcasted_iota(jnp.int32, (wide, tokens), 0) // head_dim
    ones = jnp.ones((16, count), jnp.bfloat16)
    units = [(plane, pair) for pair in range(GROUP // 2) for plane in range(planes)]
    key_rows = count // taps // cells

    def spread(pair):
        for side in range(2):
            head = group * GROUP + 2 * pair + side
            for at, tap in enumerate(which):
                line = bias_ref[pl.ds(head * kernel + tap, 1), :]
                for key_row in range(key_rows):
                    row = line[:, key_row * tokens : (key_row + 1) * tokens]
                    start = (at * key_rows + key_row) * cells
                    spread_ref[pair % 2, side, start : start + cells, :] = pltpu.roll(
                        jnp.broadcast_to(row, (cells, tokens)),
                        0,
                        1,
                        stride=y_rows,
                        stride_axis=0,
                    )

    def score(slot, plane, pair):
        if plane == 0:
            spread(pair)
        keys = keys_ref[plane, :, pl.ds(base, wide)]
        queries = query_ref[plane, pl.ds(base, wide), :].astype(jnp.float32) * scale
        chosen = []
        for side in range(2):
            one_head = jnp.where(head_of_row == 2 * pair + side, queries, 0.0)
            coarse = one_head.astype(jnp.bfloat16)
            fine = (one_head - coarse.astype(jnp.float32)).astype(jnp.bfloat16)
            chosen.append(jnp.concatenate([coarse, fine], 0))
        dotted = jnp.dot(
            jnp.concatenate([keys, keys], 1),
            jnp.concatenate(chosen, 1),
            preferred_element_type=jnp.float32,
        )
        tops = []
        for side in range(2):
            head = 2 * pair + side
            scores = dotted[:, side * tokens : (side + 1) * tokens] + spread_ref[pair % 2, side]
            score_ref[slot, side] = scores
            top = jnp.max(scores.reshape(count // CHAINS, CHAINS, tokens), axis=0)
            top = jnp.max(top, axis=0, keepdims=True)
            if not first:
                top = jnp.maximum(top, max_in[plane, pl.ds(group * GROUP + head, 1), :])
            tops.append(top)
        return tops

    def mix(slot, plane, pair, tops):
        exponents = [
            jnp.exp2(score_ref[slot, side] - tops[side]).astype(jnp.bfloat16) for side in range(2)
        ]
        start = pl.multiple_of(base + pair * 2 * head_dim, 2 * head_dim)
        values = values_ref[plane, pl.ds(start, 2 * head_dim), :]
        mixed = jnp.dot(
            jnp.concatenate([values, ones], 0),
            jnp.concatenate(exponents, 1),
            preferred_element_type=jnp.float32,
        )
        for side in range(2):
            head = 2 * pair + side
            lanes = slice(side * tokens, (side + 1) * tokens)
            acc = mixed[side * head_dim : (side + 1) * head_dim, lanes]
            total = mixed[2 * head_dim : 2 * head_dim + 1, lanes]
            rows = pl.ds(pl.multiple_of(start + side * head_dim, head_dim), head_dim)
            one = pl.ds(group * GROUP + head, 1)
            if not first:
                shrink = jnp.exp2(max_in[plane, one, :] - tops[side])
                acc = acc + acc_in[plane, rows, :] * shrink
                total = total + sum_in[plane, one, :] * shrink
            if last:
                attended_ref[plane, rows, :] = (acc / total).astype(jnp.bfloat16)
            else:
                acc_out[plane, rows, :] = acc
                max_out[plane, one, :] = tops[side]
                sum_out[plane, one, :] = total

    waiting = score(0, *units[0])
    for index, unit in enumerate(units):
        tops = waiting
        if index + 1 < len(units):
            waiting = score((index + 1) % 2, *units[index + 1])
        mix(index % 2, *unit, tops)

    if last:

        @pl.when(group == pl.num_programs(0) - 1)
        def _():
            for plane in range(planes):
                projection = lax.dot_general(
                    reorder(attended_ref[plane], 1),
                    wo_ref[...],
                    (((0,), (0,)), ((), ())),
                    preferred_element_type=jnp.float32,
                )
                mean_sq = jnp.mean(projection * projection, axis=-1, keepdims=True)
                update = projection * lax.rsqrt(mean_sq + 1e-06) * gain_ref[...]
                out_ref[plane] = update.astype(jnp.bfloat16)


def stage(which, own, low, high, wk, wv, bias, shape, first=None, state=None, last=None):
    taps = len(which)
    tokens, width = own.shape[1:]
    planes = own.shape[0] // taps
    heads, kernel, cells = shape
    y_rows = tokens // cells
    count = (y_rows + kernel - 1) * cells * taps
    head_dim = width // heads

    def whole(a):
        rank = len(a.shape)
        return pl.BlockSpec(a.shape, lambda g: (0,) * rank)

    inputs = [own, low, high, wk, wv, bias]
    specs = [whole(a) for a in inputs]
    extra = ([first] if first is not None else list(state)) + (list(last) if last else [])
    inputs += extra
    specs += [whole(a) for a in extra]
    if last:
        outs = [jax.ShapeDtypeStruct((planes, tokens, width), jnp.bfloat16)]
    else:
        outs = [
            jax.ShapeDtypeStruct((planes, width, tokens), jnp.float32),
            jax.ShapeDtypeStruct((planes, heads, tokens), jnp.float32),
            jax.ShapeDtypeStruct((planes, heads, tokens), jnp.float32),
        ]
        if first is not None:
            outs = [jax.ShapeDtypeStruct((planes, width, tokens), jnp.bfloat16)] + outs
    scratch = [
        pltpu.VMEM((planes, count, width), jnp.bfloat16),
        pltpu.VMEM((planes, width, count), jnp.bfloat16),
        pltpu.VMEM((2, 2, count, tokens), jnp.float32),
        pltpu.VMEM((2, 2, count, tokens), jnp.float32),
    ]
    if last:
        scratch.append(pltpu.VMEM((planes, width, tokens), jnp.bfloat16))
    scale = float(head_dim) ** -0.5 * LOG2E
    return pl.pallas_call(
        functools.partial(
            stage_kernel, which, kernel, cells, first is not None, last is not None, scale
        ),
        grid=(heads // GROUP,),
        in_specs=specs,
        out_specs=[whole(a) for a in outs],
        out_shape=outs,
        scratch_shapes=scratch,
        cost_estimate=pl.CostEstimate(
            flops=taps * 1_500_000_000, transcendentals=0, bytes_accessed=taps * 4_000_000
        ),
        compiler_params=pltpu.CompilerParams(vmem_limit_bytes=24 * 1024 * 1024),
    )(*inputs)


def sublayer(tokens, w_qkv, w_out, rel_bias, gain):
    boxes, depth_planes, y_rows, cells, width = tokens.shape
    heads = rel_bias.shape[0]
    head_dim = width // heads
    stride = DILATION_DEPTH // depth_planes
    own = tokens.reshape(boxes * depth_planes, y_rows * cells, width)

    below = shifted(own, "gz", stride)
    above = shifted(own, "gz", -stride)
    low = shifted(own, "gy", 1)
    high = shifted(own, "gy", -1)
    below_two = shifted(below, "gz", stride)
    above_two = shifted(above, "gz", -stride)
    near = jnp.concatenate([below, above], 0)
    near_low = shifted(near, "gy", 1)
    near_high = shifted(near, "gy", -1)
    far = jnp.concatenate([below_two, above_two], 0)
    far_low = shifted(far, "gy", 1)
    far_high = shifted(far, "gy", -1)

    wq, wk, wv = split_weights(w_qkv, head_dim)
    bias = bias_rows(rel_bias, y_rows, cells)
    shape = (heads, rel_bias.shape[1], cells)

    query, *state = stage((2,), own, low, high, wk, wv, bias, shape, first=wq)
    state = stage((1, 3), near, near_low, near_high, wk, wv, bias, shape, state=[query] + state)
    (update,) = stage(
        (0, 4),
        far,
        far_low,
        far_high,
        wk,
        wv,
        bias,
        shape,
        state=[query] + list(state),
        last=(w_out, gain.reshape(1, width)),
    )
    return update.reshape(tokens.shape)


def solution(mesh):
    in_specs = (P(None, "gz", "gy", None, None), P(), P(), P(), P())
    out_specs = P(None, "gz", "gy", None, None)
    return jax.shard_map(sublayer, mesh=mesh, in_specs=in_specs, out_specs=out_specs, check_vma=False)
```

```python
import functools
import math

import jax
import jax.numpy as jnp
import numpy as np
from jax import lax
from jax.experimental import pallas as pl
from jax.experimental.pallas import tpu as pltpu
from jax.sharding import PartitionSpec as P


DILATION_DEPTH = 8
LOG2E = math.log2(math.e)
MASKED = -1e30
GROUP = 4
CHUNK = 16
LIVE = 8


def product_nt(a, b):
    return lax.dot_general(a, b, (((1,), (1,)), ((), ())), preferred_element_type=jnp.float32)


def shifted(block, axis, distance):
    count = lax.axis_size(axis)
    return lax.ppermute(block, axis, [((i - distance) % count, i) for i in range(count)])


def weight_kernel(head_dim, w_ref, query_ref, key_ref, value_ref):
    wide = GROUP * head_dim
    rows = lax.broadcasted_iota(jnp.int32, (wide, 3 * wide), 0)
    columns = lax.broadcasted_iota(jnp.int32, (wide, 3 * wide), 1)
    for group in range(key_ref.shape[0] // wide):
        block = w_ref[:, group * 3 * wide : (group + 1) * 3 * wide]
        for kind, ref in enumerate((query_ref, key_ref, value_ref)):
            source = (rows // head_dim) * 3 * head_dim + kind * head_dim + rows % head_dim
            pick = jnp.where(columns == source, 1.0, 0.0).astype(jnp.bfloat16)
            where = slice(group * wide, (group + 1) * wide)
            if kind == 1:
                ref[:, where] = product_nt(block, pick).astype(jnp.bfloat16)
            else:
                ref[where, :] = product_nt(pick, block).astype(jnp.bfloat16)


def split_weights(w_qkv, head_dim):
    width = w_qkv.shape[0]
    one = pltpu.VMEM((width, width), jnp.bfloat16)
    return pl.pallas_call(
        functools.partial(weight_kernel, head_dim),
        out_shape=[one] * 3,
        cost_estimate=pl.CostEstimate(
            flops=3_000_000_000, transcendentals=0, bytes_accessed=3_000_000
        ),
        name="split_weights",
    )(w_qkv)


def bias_rows(rel_bias, y_rows):
    heads, taps, kernel, _ = rel_bias.shape
    key_rows = y_rows + kernel - 1
    lanes = GROUP * CHUNK * y_rows
    place = np.zeros((GROUP, kernel, kernel, key_rows, lanes), np.float32)
    for key_row in range(key_rows):
        for q in range(y_rows):
            if 0 <= key_row - q < kernel:
                for a in range(GROUP):
                    for k in range(kernel):
                        lane = ((a * CHUNK - k) * y_rows + q) % lanes
                        place[a, key_row - q, k, key_row, lane] = 1.0
    place = place.reshape(GROUP * kernel * kernel, key_rows * lanes)
    seen = place.sum(0).reshape(key_rows, GROUP * CHUNK, y_rows).max(1, keepdims=True)
    outside = np.broadcast_to(seen, (key_rows, GROUP * CHUNK, y_rows)).reshape(key_rows * lanes)
    outside = np.where(outside > 0, 0.0, MASKED).astype(np.float32)
    table = rel_bias.reshape(heads // GROUP, GROUP, taps, kernel * kernel).transpose(0, 2, 1, 3)
    rows = jnp.dot(
        table.reshape(heads // GROUP * taps, GROUP * kernel * kernel),
        jnp.asarray(place),
        precision=lax.Precision.HIGHEST,
    )
    return rows * LOG2E + jnp.asarray(outside)


def stage_kernel(layout, kernel, cells, first, last, scale, *refs):
    refs = list(refs)
    block_refs = refs[: len(layout)]
    wk_ref, wv_ref, bias_ref = refs[len(layout) : len(layout) + 3]
    refs = refs[len(layout) + 3 :]
    if first:
        wq_ref = refs.pop(0)
    else:
        query_in, acc_in, max_in, sum_in = refs[:4]
        refs = refs[4:]
    if last:
        wo_ref, gain_ref, out_ref = refs[:3]
        refs = refs[3:]
    else:
        if first:
            query_out = refs.pop(0)
        acc_out, max_out, sum_out = refs[:3]
        refs = refs[3:]
    token_ref, keys_ref, values_ref, score_ref, tail_ref, spread_ref = refs[:6]
    refs = refs[6:]
    if last:
        attended_ref, done_ref = refs
    query_ref = query_out if first else query_in
    planes = block_refs[0].shape[0] // len(layout[0])
    tokens = block_refs[0].shape[1]
    width = block_refs[0].shape[2]
    places = [place for group_of in layout for place in group_of]
    y_rows = tokens // cells
    chunks = cells // CHUNK
    wide = wk_ref.shape[1] // pl.num_programs(0)
    head_dim = wide // GROUP
    span = keys_ref.shape[2]
    rows = span // CHUNK
    group = pl.program_id(0)

    token = lax.broadcasted_iota(jnp.int32, (tokens, tokens), 0)
    lane = lax.broadcasted_iota(jnp.int32, (tokens, tokens), 1)
    lane_head = lane // (CHUNK * y_rows)
    lane_x = lane // y_rows % CHUNK
    same_head = token // head_dim == lane_head

    def chosen(chunk):
        x = (lane_x + chunk * CHUNK + kernel // 2) % cells
        return jnp.where(token == lane % y_rows * cells + x, 1.0, 0.0).astype(jnp.bfloat16)

    @pl.when(group == 0)
    def _():
        at = 0
        for group_of, ref in zip(layout, block_refs):
            for tap in range(len(group_of)):
                for plane in range(planes):
                    for q in range(y_rows):
                        for chunk in range(chunks):
                            start = (chunk * rows + at * y_rows + q) * CHUNK
                            source = q * cells + chunk * CHUNK
                            token_ref[plane, start : start + CHUNK, :] = ref[
                                tap * planes + plane, source : source + CHUNK, :
                            ]
                at += 1
        for plane in range(planes):
            keys = jnp.dot(token_ref[plane], wk_ref[...], preferred_element_type=jnp.float32)
            keys_ref[plane] = keys.astype(jnp.bfloat16).reshape(chunks, span, width)
            step = chunks if span % 128 == 0 else 1
            for chunk in range(0, chunks, step):
                part = token_ref[plane, chunk * span : (chunk + step) * span, :]
                values = product_nt(wv_ref[...], part).astype(jnp.bfloat16)
                for more in range(step):
                    values_ref[plane, chunk + more] = values[:, more * span : (more + 1) * span]
        if first:
            own = block_refs[0][...].reshape(planes * tokens, width)
            queries = product_nt(wq_ref[...], own).astype(jnp.bfloat16)
            for plane in range(planes):
                mine = queries[:, plane * tokens : (plane + 1) * tokens]
                for chunk in range(chunks):
                    spread = jnp.dot(mine, chosen(chunk), preferred_element_type=jnp.float32)
                    for g in range(width // wide):
                        one = jnp.where(same_head, spread[g * wide : (g + 1) * wide] * scale, 0.0)
                        coarse = one.astype(jnp.bfloat16)
                        fine = (one - coarse.astype(jnp.float32)).astype(jnp.bfloat16)
                        query_out[g, plane * chunks + chunk, :wide, :] = coarse
                        query_out[g, plane * chunks + chunk, wide:, :] = fine

    for at, (tap, part) in enumerate(places):
        line = bias_ref[pl.ds(group * kernel + tap, 1), :]
        for q in range(y_rows):
            first_lane = (part * y_rows + q) * tokens
            row = jnp.broadcast_to(line[:, first_lane : first_lane + tokens], (8, tokens))
            row = pltpu.roll(row, 0, 1, stride=y_rows, stride_axis=0)
            for up in range(0, CHUNK + LIVE, 8):
                turned = pltpu.roll(row, up * y_rows, 1) if up else row
                reach = token[:8] + up - lane_x[:8]
                inside = jnp.logical_and(reach >= 0, reach < kernel)
                spread_ref[at * y_rows + q, up : up + 8, :] = jnp.where(inside, turned, MASKED)

    base = pl.multiple_of(group * wide, wide)
    ones = jnp.ones((16, span), jnp.bfloat16)
    units = [(plane, chunk) for plane in range(planes) for chunk in range(chunks)]

    def score(slot, plane, chunk):
        unit = plane * chunks + chunk
        queries = query_ref[group, unit]
        tops = []
        keys = jnp.concatenate(
            [
                keys_ref[plane, (chunk + half) % chunks, :, pl.ds(base, wide)]
                for half in range(2)
            ],
            0,
        )
        both = jnp.dot(
            jnp.concatenate([keys, keys], 1), queries, preferred_element_type=jnp.float32
        )
        for half in range(2):
            dotted = both[half * span : (half + 1) * span].reshape(rows, CHUNK, tokens)
            if half:
                scores = dotted[:, :LIVE] + spread_ref[:, CHUNK:, :]
                tail_ref[slot] = scores
            else:
                scores = dotted + spread_ref[:, :CHUNK, :]
                score_ref[slot] = scores
            tops.append(jnp.max(scores, axis=0))
        top = jnp.maximum(jnp.maximum(tops[0][:8], tops[0][8:]), tops[1])
        top = jnp.max(top, axis=0, keepdims=True)
        if not first:
            top = jnp.maximum(top, max_in[group, unit : unit + 1, :])
        return top

    def mix(slot, plane, chunk, top):
        unit = plane * chunks + chunk
        weights, values = [], []
        for half in range(2):
            if half:
                exponents = jnp.exp2(tail_ref[slot] - top)
                exponents = jnp.concatenate([exponents, jnp.zeros_like(exponents)], 1)
            else:
                exponents = jnp.exp2(score_ref[slot] - top)
            weights.append(exponents.reshape(span, tokens).astype(jnp.bfloat16))
            part = values_ref[plane, (chunk + half) % chunks, pl.ds(base, wide), :]
            values.append(jnp.concatenate([part, ones], 0))
        if span % 128 == 0:
            weights, values = [jnp.concatenate(weights, 0)], [jnp.concatenate(values, 1)]
        mixed = sum(
            jnp.dot(v, w, preferred_element_type=jnp.float32) for v, w in zip(values, weights)
        )
        acc = mixed[:head_dim]
        for head in range(1, GROUP):
            acc = jnp.where(
                lane_head[:head_dim] == head, mixed[head * head_dim : (head + 1) * head_dim], acc
            )
        total = mixed[wide : wide + 1]
        held = slice(unit * head_dim, (unit + 1) * head_dim)
        one = slice(unit, unit + 1)
        if not first:
            shrink = jnp.exp2(max_in[group, one, :] - top)
            acc = acc + acc_in[group, held, :] * shrink
            total = total + sum_in[group, one, :] * shrink
        if last:
            done_ref[group, held, :] = acc / total
            return
        acc_out[group, held, :] = acc
        max_out[group, one, :] = top
        sum_out[group, one, :] = total

    tops = [score(slot, *unit) for slot, unit in enumerate(units)]
    for slot, unit in enumerate(units):
        mix(slot, *unit, tops[slot])

    if last:

        @pl.when(group == pl.num_programs(0) - 1)
        def _():
            order = jnp.concatenate([chosen(chunk) for chunk in range(chunks)], 1)
            for plane in range(planes):
                laid = []
                for g in range(width // wide):
                    line = []
                    for chunk in range(chunks):
                        start = (plane * chunks + chunk) * head_dim
                        mine = jnp.concatenate([done_ref[g, start : start + head_dim, :]] * GROUP, 0)
                        line.append(jnp.where(same_head, mine, 0.0).astype(jnp.bfloat16))
                    laid.append(jnp.concatenate(line, 1))
                own_rows = slice(plane * tokens, (plane + 1) * tokens)
                attended_ref[own_rows, :] = product_nt(order, jnp.concatenate(laid, 0)).astype(
                    jnp.bfloat16
                )
            projection = jnp.dot(
                attended_ref[...], wo_ref[...], preferred_element_type=jnp.float32
            )
            mean_sq = jnp.mean(projection * projection, axis=-1, keepdims=True)
            update = projection * lax.rsqrt(mean_sq + 1e-06) * gain_ref[...]
            out_ref[...] = update.astype(jnp.bfloat16).reshape(planes, tokens, width)


def stage(layout, blocks, wk, wv, bias, shape, first=None, state=None, last=None):
    tokens, width = blocks[0].shape[1:]
    planes = blocks[0].shape[0] // len(layout[0])
    heads, kernel, cells = shape
    total = sum(len(group_of) for group_of in layout)
    rows = total * (tokens // cells)
    span = rows * CHUNK
    chunks = cells // CHUNK
    groups = heads // GROUP
    head_dim = width // heads
    wide = GROUP * head_dim

    def whole(a):
        rank = len(a.shape)
        return pl.BlockSpec(a.shape, lambda g: (0,) * rank)

    inputs = list(blocks) + [wk, wv, bias]
    inputs += ([first] if first is not None else list(state)) + (list(last) if last else [])
    specs = [whole(a) for a in inputs]
    if last:
        outs = [jax.ShapeDtypeStruct((planes, tokens, width), jnp.bfloat16)]
    else:
        units = planes * chunks
        outs = [
            jax.ShapeDtypeStruct((groups, units * head_dim, tokens), jnp.float32),
            jax.ShapeDtypeStruct((groups, units, tokens), jnp.float32),
            jax.ShapeDtypeStruct((groups, units, tokens), jnp.float32),
        ]
        if first is not None:
            outs = [jax.ShapeDtypeStruct((groups, units, 2 * wide, tokens), jnp.bfloat16)] + outs
    scratch = [
        pltpu.VMEM((planes, chunks * span, width), jnp.bfloat16),
        pltpu.VMEM((planes, chunks, span, width), jnp.bfloat16),
        pltpu.VMEM((planes, chunks, width, span), jnp.bfloat16),
        pltpu.VMEM((planes * chunks, rows, CHUNK, tokens), jnp.float32),
        pltpu.VMEM((planes * chunks, rows, LIVE, tokens), jnp.float32),
        pltpu.VMEM((rows, CHUNK + LIVE, tokens), jnp.float32),
    ]
    if last:
        scratch.append(pltpu.VMEM((planes * tokens, width), jnp.bfloat16))
        scratch.append(pltpu.VMEM((groups, planes * chunks * head_dim, tokens), jnp.float32))
    scale = float(head_dim) ** -0.5 * LOG2E
    return pl.pallas_call(
        functools.partial(
            stage_kernel, layout, kernel, cells, first is not None, last is not None, scale
        ),
        grid=(groups,),
        in_specs=specs,
        out_specs=[whole(a) for a in outs],
        out_shape=outs,
        scratch_shapes=scratch,
        cost_estimate=pl.CostEstimate(
            flops=total * 500_000_000, transcendentals=0, bytes_accessed=total * 1_300_000
        ),
        compiler_params=pltpu.CompilerParams(vmem_limit_bytes=28 * 1024 * 1024),
    )(*inputs)


def sublayer(tokens, w_qkv, w_out, rel_bias, gain):
    boxes, depth_planes, y_rows, cells, width = tokens.shape
    heads = rel_bias.shape[0]
    head_dim = width // heads
    stride = DILATION_DEPTH // depth_planes
    own = tokens.reshape(boxes * depth_planes, y_rows * cells, width)

    below = shifted(own, "gz", stride)
    above = shifted(own, "gz", -stride)
    low = shifted(own, "gy", 1)
    high = shifted(own, "gy", -1)
    below_two = shifted(below, "gz", stride)
    above_two = shifted(above, "gz", -stride)
    near = jnp.concatenate([below, above], 0)
    near_low = shifted(near, "gy", 1)
    near_high = shifted(near, "gy", -1)
    far = jnp.concatenate([below_two, above_two], 0)
    far_low = shifted(far, "gy", 1)
    far_high = shifted(far, "gy", -1)

    wq, wk, wv = split_weights(w_qkv, head_dim)
    bias = bias_rows(rel_bias, y_rows)
    shape = (heads, rel_bias.shape[1], cells)

    given = (wk, wv, bias, shape)
    query, *state = stage(
        (((2, 1),), ((2, 0),), ((2, 2),), ((1, 1), (3, 1))),
        (own, low, high, near),
        *given,
        first=wq,
    )
    state = stage(
        (((1, 0), (3, 0)), ((1, 2), (3, 2)), ((0, 1), (4, 1))),
        (near_low, near_high, far),
        *given,
        state=[query] + state,
    )
    (update,) = stage(
        (((0, 0), (4, 0)), ((0, 2), (4, 2))),
        (far_low, far_high),
        *given,
        state=[query] + list(state),
        last=(w_out, gain.reshape(1, width)),
    )
    return update.reshape(tokens.shape)


def solution(mesh):
    in_specs = (P(None, "gz", "gy", None, None), P(), P(), P(), P())
    out_specs = P(None, "gz", "gy", None, None)
    return jax.shard_map(sublayer, mesh=mesh, in_specs=in_specs, out_specs=out_specs, check_vma=False)
```

```python
import functools
import math

import jax
import jax.numpy as jnp
import numpy as np
from jax import lax
from jax.experimental import pallas as pl
from jax.experimental.pallas import tpu as pltpu
from jax.sharding import PartitionSpec as P


DILATION_DEPTH = 8
LOG2E = math.log2(math.e)
MASKED = -1e30
GROUP = 4
CHUNK = 16
LIVE = 8


def product_nt(a, b):
    return lax.dot_general(a, b, (((1,), (1,)), ((), ())), preferred_element_type=jnp.float32)


def shifted(block, axis, distance):
    count = lax.axis_size(axis)
    return lax.ppermute(block, axis, [((i - distance) % count, i) for i in range(count)])


def weight_kernel(head_dim, w_ref, query_ref, key_ref, value_ref):
    wide = GROUP * head_dim
    rows = lax.broadcasted_iota(jnp.int32, (wide, 3 * wide), 0)
    columns = lax.broadcasted_iota(jnp.int32, (wide, 3 * wide), 1)
    for group in range(key_ref.shape[0] // wide):
        block = w_ref[:, group * 3 * wide : (group + 1) * 3 * wide]
        for kind, ref in enumerate((query_ref, key_ref, value_ref)):
            source = (rows // head_dim) * 3 * head_dim + kind * head_dim + rows % head_dim
            pick = jnp.where(columns == source, 1.0, 0.0).astype(jnp.bfloat16)
            where = slice(group * wide, (group + 1) * wide)
            if kind == 1:
                ref[:, where] = product_nt(block, pick).astype(jnp.bfloat16)
            else:
                ref[where, :] = product_nt(pick, block).astype(jnp.bfloat16)


def split_weights(w_qkv, head_dim):
    width = w_qkv.shape[0]
    one = pltpu.VMEM((width, width), jnp.bfloat16)
    return pl.pallas_call(
        functools.partial(weight_kernel, head_dim),
        out_shape=[one] * 3,
        cost_estimate=pl.CostEstimate(
            flops=3_000_000_000, transcendentals=0, bytes_accessed=3_000_000
        ),
        name="split_weights",
    )(w_qkv)


def bias_rows(rel_bias, y_rows):
    heads, taps, kernel, _ = rel_bias.shape
    key_rows = y_rows + kernel - 1
    lanes = GROUP * CHUNK * y_rows
    place = np.zeros((GROUP, kernel, kernel, key_rows, lanes), np.float32)
    for key_row in range(key_rows):
        for q in range(y_rows):
            if 0 <= key_row - q < kernel:
                for a in range(GROUP):
                    for k in range(kernel):
                        lane = ((a * CHUNK - k) * y_rows + q) % lanes
                        place[a, key_row - q, k, key_row, lane] = 1.0
    place = place.reshape(GROUP * kernel * kernel, key_rows * lanes)
    seen = place.sum(0).reshape(key_rows, GROUP * CHUNK, y_rows).max(1, keepdims=True)
    outside = np.broadcast_to(seen, (key_rows, GROUP * CHUNK, y_rows)).reshape(key_rows * lanes)
    outside = np.where(outside > 0, 0.0, MASKED).astype(np.float32)
    table = rel_bias.reshape(heads // GROUP, GROUP, taps, kernel * kernel).transpose(0, 2, 1, 3)
    rows = jnp.dot(
        table.reshape(heads // GROUP * taps, GROUP * kernel * kernel),
        jnp.asarray(place),
        precision=lax.Precision.HIGHEST,
    )
    return rows * LOG2E + jnp.asarray(outside)


def stage_kernel(layout, kernel, cells, first, last, scale, *refs):
    refs = list(refs)
    block_refs = refs[: len(layout)]
    wk_ref, wv_ref, bias_ref = refs[len(layout) : len(layout) + 3]
    refs = refs[len(layout) + 3 :]
    if first:
        wq_ref = refs.pop(0)
    else:
        query_in, acc_in, max_in, sum_in = refs[:4]
        refs = refs[4:]
    if last:
        wo_ref, gain_ref, out_ref = refs[:3]
        refs = refs[3:]
    else:
        if first:
            query_out = refs.pop(0)
        acc_out, max_out, sum_out = refs[:3]
        refs = refs[3:]
    token_ref, keys_ref, values_ref, score_ref, tail_ref, spread_ref = refs[:6]
    refs = refs[6:]
    if last:
        attended_ref, done_ref = refs
    query_ref = query_out if first else query_in
    planes = block_refs[0].shape[0] // len(layout[0])
    tokens = block_refs[0].shape[1]
    width = block_refs[0].shape[2]
    places = [place for group_of in layout for place in group_of]
    y_rows = tokens // cells
    chunks = cells // CHUNK
    wide = wk_ref.shape[1] // pl.num_programs(0)
    head_dim = wide // GROUP
    span = keys_ref.shape[2]
    rows = span // CHUNK
    group = pl.program_id(0)

    token = lax.broadcasted_iota(jnp.int32, (tokens, tokens), 0)
    lane = lax.broadcasted_iota(jnp.int32, (tokens, tokens), 1)
    lane_head = lane // (CHUNK * y_rows)
    lane_x = lane // y_rows % CHUNK
    same_head = token // head_dim == lane_head

    def chosen(chunk):
        x = (lane_x + chunk * CHUNK + kernel // 2) % cells
        return jnp.where(token == lane % y_rows * cells + x, 1.0, 0.0).astype(jnp.bfloat16)

    @pl.when(group == 0)
    def _():
        at = 0
        for group_of, ref in zip(layout, block_refs):
            for tap in range(len(group_of)):
                for plane in range(planes):
                    for q in range(y_rows):
                        for chunk in range(chunks):
                            start = (chunk * rows + at * y_rows + q) * CHUNK
                            source = q * cells + chunk * CHUNK
                            token_ref[plane, start : start + CHUNK, :] = ref[
                                tap * planes + plane, source : source + CHUNK, :
                            ]
                at += 1
        for plane in range(planes):
            keys = jnp.dot(token_ref[plane], wk_ref[...], preferred_element_type=jnp.float32)
            keys_ref[plane] = keys.astype(jnp.bfloat16).reshape(chunks, span, width)
            step = chunks if span % 128 == 0 else 1
            for chunk in range(0, chunks, step):
                part = token_ref[plane, chunk * span : (chunk + step) * span, :]
                values = product_nt(wv_ref[...], part).astype(jnp.bfloat16)
                for more in range(step):
                    values_ref[plane, chunk + more] = values[:, more * span : (more + 1) * span]
        if first:
            own = block_refs[0][...].reshape(planes * tokens, width)
            queries = product_nt(wq_ref[...], own).astype(jnp.bfloat16)
            for plane in range(planes):
                mine = queries[:, plane * tokens : (plane + 1) * tokens]
                for chunk in range(chunks):
                    spread = jnp.dot(mine, chosen(chunk), preferred_element_type=jnp.float32)
                    for g in range(width // wide):
                        one = jnp.where(same_head, spread[g * wide : (g + 1) * wide] * scale, 0.0)
                        coarse = one.astype(jnp.bfloat16)
                        fine = (one - coarse.astype(jnp.float32)).astype(jnp.bfloat16)
                        query_out[g, plane * chunks + chunk, :wide, :] = coarse
                        query_out[g, plane * chunks + chunk, wide:, :] = fine

    for at, (tap, part) in enumerate(places):
        line = bias_ref[pl.ds(group * kernel + tap, 1), :]
        for q in range(y_rows):
            first_lane = (part * y_rows + q) * tokens
            row = jnp.broadcast_to(line[:, first_lane : first_lane + tokens], (8, tokens))
            row = pltpu.roll(row, 0, 1, stride=y_rows, stride_axis=0)
            for up in range(0, CHUNK + LIVE, 8):
                turned = pltpu.roll(row, up * y_rows, 1) if up else row
                reach = token[:8] + up - lane_x[:8]
                inside = jnp.logical_and(reach >= 0, reach < kernel)
                spread_ref[at * y_rows + q, up : up + 8, :] = jnp.where(inside, turned, MASKED)

    base = pl.multiple_of(group * wide, wide)
    ones = jnp.ones((16, span), jnp.bfloat16)
    units = [(plane, chunk) for plane in range(planes) for chunk in range(chunks)]

    def score(slot, plane, chunk):
        unit = plane * chunks + chunk
        queries = query_ref[group, unit]
        tops = []
        keys = jnp.concatenate(
            [
                keys_ref[plane, (chunk + half) % chunks, :, pl.ds(base, wide)]
                for half in range(2)
            ],
            0,
        )
        both = jnp.dot(
            jnp.concatenate([keys, keys], 1), queries, preferred_element_type=jnp.float32
        )
        for half in range(2):
            dotted = both[half * span : (half + 1) * span].reshape(rows, CHUNK, tokens)
            if half:
                scores = dotted[:, :LIVE] + spread_ref[:, CHUNK:, :]
                tail_ref[slot] = scores
            else:
                scores = dotted + spread_ref[:, :CHUNK, :]
                score_ref[slot] = scores
            tops.append(jnp.max(scores, axis=0))
        top = jnp.maximum(jnp.maximum(tops[0][:8], tops[0][8:]), tops[1])
        top = jnp.max(top, axis=0, keepdims=True)
        if not first:
            top = jnp.maximum(top, max_in[group, unit : unit + 1, :])
        return top

    def mix(slot, plane, chunk, top):
        unit = plane * chunks + chunk
        weights, values = [], []
        for half in range(2):
            if half:
                exponents = jnp.exp2(tail_ref[slot] - top)
                exponents = jnp.concatenate([exponents, jnp.zeros_like(exponents)], 1)
            else:
                exponents = jnp.exp2(score_ref[slot] - top)
            weights.append(exponents.reshape(span, tokens).astype(jnp.bfloat16))
            part = values_ref[plane, (chunk + half) % chunks, pl.ds(base, wide), :]
            values.append(jnp.concatenate([part, ones], 0))
        if span % 128 == 0:
            weights, values = [jnp.concatenate(weights, 0)], [jnp.concatenate(values, 1)]
        mixed = sum(
            jnp.dot(v, w, preferred_element_type=jnp.float32) for v, w in zip(values, weights)
        )
        acc = mixed[:head_dim]
        for head in range(1, GROUP):
            acc = jnp.where(
                lane_head[:head_dim] == head, mixed[head * head_dim : (head + 1) * head_dim], acc
            )
        total = mixed[wide : wide + 1]
        held = slice(unit * head_dim, (unit + 1) * head_dim)
        one = slice(unit, unit + 1)
        if not first:
            shrink = jnp.exp2(max_in[group, one, :] - top)
            acc = acc + acc_in[group, held, :] * shrink
            total = total + sum_in[group, one, :] * shrink
        if last:
            done_ref[group, held, :] = acc / total
            return
        acc_out[group, held, :] = acc
        max_out[group, one, :] = top
        sum_out[group, one, :] = total

    tops = [score(slot, *unit) for slot, unit in enumerate(units)]
    for slot, unit in enumerate(units):
        mix(slot, *unit, tops[slot])

    if last:

        @pl.when(group == pl.num_programs(0) - 1)
        def _():
            order = jnp.concatenate([chosen(chunk) for chunk in range(chunks)], 1)
            for plane in range(planes):
                laid = []
                for g in range(width // wide):
                    line = []
                    for chunk in range(chunks):
                        start = (plane * chunks + chunk) * head_dim
                        mine = jnp.concatenate([done_ref[g, start : start + head_dim, :]] * GROUP, 0)
                        line.append(jnp.where(same_head, mine, 0.0).astype(jnp.bfloat16))
                    laid.append(jnp.concatenate(line, 1))
                own_rows = slice(plane * tokens, (plane + 1) * tokens)
                attended_ref[own_rows, :] = product_nt(order, jnp.concatenate(laid, 0)).astype(
                    jnp.bfloat16
                )
            projection = jnp.dot(
                attended_ref[...], wo_ref[...], preferred_element_type=jnp.float32
            )
            mean_sq = jnp.mean(projection * projection, axis=-1, keepdims=True)
            update = projection * lax.rsqrt(mean_sq + 1e-06) * gain_ref[...]
            out_ref[...] = update.astype(jnp.bfloat16).reshape(planes, tokens, width)


def stage(layout, blocks, wk, wv, bias, shape, first=None, state=None, last=None):
    tokens, width = blocks[0].shape[1:]
    planes = blocks[0].shape[0] // len(layout[0])
    heads, kernel, cells = shape
    total = sum(len(group_of) for group_of in layout)
    rows = total * (tokens // cells)
    span = rows * CHUNK
    chunks = cells // CHUNK
    groups = heads // GROUP
    head_dim = width // heads
    wide = GROUP * head_dim

    def whole(a):
        rank = len(a.shape)
        return pl.BlockSpec(a.shape, lambda g: (0,) * rank)

    inputs = list(blocks) + [wk, wv, bias]
    inputs += ([first] if first is not None else list(state)) + (list(last) if last else [])
    specs = [whole(a) for a in inputs]
    if last:
        outs = [jax.ShapeDtypeStruct((planes, tokens, width), jnp.bfloat16)]
    else:
        units = planes * chunks
        outs = [
            jax.ShapeDtypeStruct((groups, units * head_dim, tokens), jnp.float32),
            jax.ShapeDtypeStruct((groups, units, tokens), jnp.float32),
            jax.ShapeDtypeStruct((groups, units, tokens), jnp.float32),
        ]
        if first is not None:
            outs = [jax.ShapeDtypeStruct((groups, units, 2 * wide, tokens), jnp.bfloat16)] + outs
    scratch = [
        pltpu.VMEM((planes, chunks * span, width), jnp.bfloat16),
        pltpu.VMEM((planes, chunks, span, width), jnp.bfloat16),
        pltpu.VMEM((planes, chunks, width, span), jnp.bfloat16),
        pltpu.VMEM((planes * chunks, rows, CHUNK, tokens), jnp.float32),
        pltpu.VMEM((planes * chunks, rows, LIVE, tokens), jnp.float32),
        pltpu.VMEM((rows, CHUNK + LIVE, tokens), jnp.float32),
    ]
    if last:
        scratch.append(pltpu.VMEM((planes * tokens, width), jnp.bfloat16))
        scratch.append(pltpu.VMEM((groups, planes * chunks * head_dim, tokens), jnp.float32))
    scale = float(head_dim) ** -0.5 * LOG2E
    return pl.pallas_call(
        functools.partial(
            stage_kernel, layout, kernel, cells, first is not None, last is not None, scale
        ),
        grid=(groups,),
        in_specs=specs,
        out_specs=[whole(a) for a in outs],
        out_shape=outs,
        scratch_shapes=scratch,
        cost_estimate=pl.CostEstimate(
            flops=total * 500_000_000, transcendentals=0, bytes_accessed=total * 1_300_000
        ),
        compiler_params=pltpu.CompilerParams(vmem_limit_bytes=28 * 1024 * 1024),
    )(*inputs)


def sublayer(tokens, w_qkv, w_out, rel_bias, gain):
    boxes, depth_planes, y_rows, cells, width = tokens.shape
    heads = rel_bias.shape[0]
    head_dim = width // heads
    stride = DILATION_DEPTH // depth_planes
    own = tokens.reshape(boxes * depth_planes, y_rows * cells, width)

    below = shifted(own, "gz", stride)
    above = shifted(own, "gz", -stride)
    low = shifted(own, "gy", 1)
    high = shifted(own, "gy", -1)
    below_two = shifted(below, "gz", stride)
    above_two = shifted(above, "gz", -stride)
    near = jnp.concatenate([below, above], 0)
    near_low = shifted(near, "gy", 1)
    near_high = shifted(near, "gy", -1)
    far = jnp.concatenate([below_two, above_two], 0)
    far_low = shifted(far, "gy", 1)
    far_high = shifted(far, "gy", -1)

    wq, wk, wv = split_weights(w_qkv, head_dim)
    bias = bias_rows(rel_bias, y_rows)
    shape = (heads, rel_bias.shape[1], cells)

    given = (wk, wv, bias, shape)
    query, *state = stage(
        (((2, 1),), ((2, 0),), ((2, 2),)),
        (own, low, high),
        *given,
        first=wq,
    )
    state = stage(
        (((1, 0), (3, 0)), ((1, 2), (3, 2)), ((0, 1), (4, 1)), ((1, 1), (3, 1))),
        (near_low, near_high, far, near),
        *given,
        state=[query] + state,
    )
    (update,) = stage(
        (((0, 0), (4, 0)), ((0, 2), (4, 2))),
        (far_low, far_high),
        *given,
        state=[query] + list(state),
        last=(w_out, gain.reshape(1, width)),
    )
    return update.reshape(tokens.shape)


def solution(mesh):
    in_specs = (P(None, "gz", "gy", None, None), P(), P(), P(), P())
    out_specs = P(None, "gz", "gy", None, None)
    return jax.shard_map(sublayer, mesh=mesh, in_specs=in_specs, out_specs=out_specs, check_vma=False)
```
